32 devices in a mesh: section: 4 (over x, core), blk: 4 (over z), tp: 2 (over y).
Axes of the slice: x: 2, y: 2, z: 4, core: 2. Of those that a mesh axis runs over, the one named last changes fastest.
Arguments:
- query: bfloat16 [2048, 8192], P(('section', 'blk'), 'tp'), may hold values from -6 to 6
- text_frame: int32 [2048], P(('section', 'blk')), may hold values from 0 to 63
- image_feats: bfloat16 [1024, 8192], P('blk', ('section', 'tp')), may hold values from -6 to 6
- image_frame: int32 [1024], P('blk'), may hold values from 0 to 63, never falling along the last dimension, each value on 1 to 32 neighbouring positions
- kv_weight: bfloat16 [4, 8192, 2, 1024], P('section', None, None, 'tp'), may hold values from -0.0625 to 0.0625
- query_gain: float32 [4, 128], P('section'), may hold values from 0.1 to 1.9
- key_gain: float32 [4, 128], P('section'), may hold values from 0.1 to 1.9
Outputs:
- attended: bfloat16 [2048, 8192], P(('section', 'blk'), 'tp')
The draws below stay inside these ranges and needn't reach their ends.
Inputs may be any that keep to these rules, and one draw needn't show every extreme that they name: `image_frame`: image frame ids never fall along the image tokens; every frame has at least one token.
All inputs are finite; a program needn't handle non-finite values.
Results may differ from the reference program's by a relative error of at most 0.007.
Values may be sent and summed in bfloat16 or wider, within the bound.
A program may use at most 128 MiB of HBM per device.

```python
import math
import jax
import jax.numpy as jnp
import numpy as np
from jax import lax

HEADS = 64
KV_HEADS = 8
HEAD = 128
VW = 8192
FRAMES = 64
IMG = 1024
TEXT = 2048
SECTIONS = 4
N_SECTION = 4


def set_ends(entries, stream_key, low, largest):
    dims = entries.shape
    spot = [jax.random.randint(jax.random.fold_in(stream_key, axis), (), 0, dims[axis]) for axis in range(len(dims))]
    entries = entries.at[tuple(spot)].set(low)
    longest = dims.index(max(dims))
    spot[longest] = (spot[longest] + 1) % dims[longest]
    return entries.at[tuple(spot)].set(largest)


def steps_of(stream_key, dims, split, low, largest):
    def one(position, blocks):
        draws = jax.random.uniform(jax.random.fold_in(jax.random.fold_in(stream_key, 6), position), (blocks,), jnp.float32, low / len(split), largest / len(split))
        return jnp.repeat(jnp.exp(draws), dims[position] // blocks).reshape((-1,) + (1,) * (len(dims) - position - 1))

    factor_of = one(*split[0])
    for cut in split[1:]:
        factor_of = factor_of * one(*cut)
    return factor_of


def length_profile(count, total, reach, slope):
    weights = [(1 << 20) // math.isqrt(standing ** slope) + 1 for standing in range(2, count + 1)]
    spare, counts = total - reach - (count - 1), [1] * (count - 1)
    while spare > 0:
        free = [i for i in range(count - 1) if counts[i] < reach]
        whole, budget = sum([weights[i] for i in free]), spare
        for i in free:
            extra = min(reach - counts[i], max(1, budget * weights[i] // whole), spare)
            counts[i] = counts[i] + extra
            spare = spare - extra
    return np.array([reach] + counts)


def ragged_sizes(key, count, total, bound, skew):
    if count == 2:
        one = jax.random.randint(key, (), max(1, total - bound), min(bound, total - 1) + 1)
        return jnp.stack([one, total - one])
    lengths = jnp.asarray(length_profile(count, total, bound, skew), jnp.int32)
    pairs = (count - 1) // 2
    donor, taker = lengths[1:1 + 2 * pairs:2], lengths[2:2 + 2 * pairs:2]
    room = jnp.minimum(donor - 1, bound - taker)
    shifted = jax.random.randint(jax.random.fold_in(key, 1), (pairs,), 0, 1 << 20) % (room + 1)
    lengths = lengths.at[1:1 + 2 * pairs:2].set(donor - shifted).at[2:2 + 2 * pairs:2].set(taker + shifted)
    return lengths[jax.random.permutation(jax.random.fold_in(key, 2), count)]


def centred(rng, dims, deviation, limit, shards=(), kind=jnp.bfloat16):
    entries = jax.random.normal(rng, dims, jnp.float32) * deviation
    if len(shards) > 0:
        entries = steps_of(rng, dims, shards, -0.22, 0.18) * entries
    return jnp.clip(entries, min=-limit, max=limit).astype(kind)


def setup_inputs(seed: int = 0) -> dict:
    key_of = jax.random.split(jax.random.key(seed), 8)
    query = centred(key_of[0], (TEXT, HEADS * HEAD), 1.0, 6.0, ((0, 16), (1, 2)))
    text_frame = set_ends(jax.random.randint(key_of[1], (TEXT,), 0, FRAMES), jax.random.fold_in(key_of[1], 1), 0, FRAMES - 1).astype(jnp.int32)
    image_feats = centred(key_of[2], (IMG, VW), 1.0, 6.0, ((0, 4), (1, 8)))
    image_frame = jnp.searchsorted(jnp.cumsum(ragged_sizes(key_of[3], FRAMES, IMG, 2 * IMG // FRAMES, 0)), jnp.arange(IMG), side="right").astype(jnp.int32)
    kv_weight = centred(key_of[4], (SECTIONS, VW, 2, KV_HEADS * HEAD), VW ** -0.5, 0.0625, ((0, 4), (3, 2)))
    query_gain = jnp.clip(1.0 + 0.18 * jax.random.normal(key_of[5], (SECTIONS, HEAD), jnp.float32), 0.1, 1.9)
    key_gain = jnp.clip(1.0 + 0.18 * jax.random.normal(key_of[6], (SECTIONS, HEAD), jnp.float32), 0.1, 1.9)
    return dict(query=query, text_frame=text_frame, image_feats=image_feats, image_frame=image_frame, kv_weight=kv_weight, query_gain=query_gain, key_gain=key_gain)


def normalize(x):
    return x * lax.rsqrt(lax.optimization_barrier(jnp.mean(x * x, axis=-1, keepdims=True)) + 1e-05)

def one_head(q, k, v, allowed):
    scores = jnp.einsum('tgd,sd->gts', q.astype(jnp.float32), k.astype(jnp.float32))
    weights = jnp.where(allowed[None], jnp.exp(scores), jnp.float32(0.0))
    total = lax.optimization_barrier(jnp.sum(weights, axis=-1, keepdims=True))
    wb = weights.astype(jnp.bfloat16)
    summed = jnp.einsum('gts,sd->gtd', wb.astype(jnp.float32), v.astype(jnp.float32))
    return summed / total

def reference(query, text_frame, image_feats, image_frame, kv_weight, query_gain, key_gain):
    rows = TEXT // N_SECTION
    groups = HEADS // KV_HEADS
    outputs = []
    for section_id in range(N_SECTION):
        weight = kv_weight[section_id].reshape(VW, 2 * KV_HEADS * HEAD)
        proj = jnp.dot(image_feats, weight, preferred_element_type=jnp.float32).reshape(IMG, 2, KV_HEADS, HEAD)
        keys = (normalize(proj[:, 0]) * key_gain[section_id]).astype(jnp.bfloat16)
        values = proj[:, 1].astype(jnp.bfloat16)
        qrows = query[section_id * rows:(section_id + 1) * rows].astype(jnp.float32).reshape(rows, KV_HEADS, groups, HEAD)
        qn = (normalize(qrows) * query_gain[section_id] * HEAD ** (-0.5)).astype(jnp.bfloat16)
        frames = text_frame[section_id * rows:(section_id + 1) * rows]
        allowed = image_frame[None, :] <= frames[:, None]
        result = lax.map(lambda item: one_head(item[0], item[1], item[2], allowed), (qn.transpose(1, 0, 2, 3), keys.transpose(1, 0, 2), values.transpose(1, 0, 2)))
        outputs.append(result.transpose(2, 0, 1, 3).reshape(rows, HEADS * HEAD).astype(jnp.bfloat16))
    return jnp.concatenate(outputs, axis=0)
```

```python
import jax
import jax.numpy as jnp
from jax import lax
from jax.sharding import PartitionSpec as P


def normalize(x):
    return x * lax.rsqrt(jnp.mean(x * x, axis=-1, keepdims=True) + 1e-05)


def per_device(query, text_frame, image_feats, image_frame, kv_weight, query_gain, key_gain):
    head_size = query_gain.shape[1]
    kv_cols = kv_weight.shape[3]
    heads_kv = kv_cols // head_size
    text_rows = query.shape[0]
    groups = query.shape[1] // kv_cols
    block_rows = image_feats.shape[0]
    wide = lax.all_gather(image_feats, ("section", "tp"), axis=1, tiled=True)
    proj = jnp.einsum("rf,fkc->krc", wide, kv_weight[0], preferred_element_type=jnp.float32)
    proj = proj.reshape(2, block_rows, heads_kv, head_size)
    keys = (normalize(proj[0]) * key_gain[0]).astype(jnp.bfloat16)
    values = proj[1].astype(jnp.bfloat16)
    key_value = jnp.stack([keys, values], axis=1).reshape(block_rows, 2, kv_cols)
    qrows = query.astype(jnp.float32).reshape(text_rows, heads_kv, groups, head_size)
    qn = (normalize(qrows) * query_gain[0] * head_size ** (-0.5)).astype(jnp.bfloat16)
    block = lax.all_gather(key_value, "blk", axis=0, tiled=True)
    frames = lax.all_gather(image_frame, "blk", axis=0, tiled=True)
    count = block.shape[0]
    keys_part = block[:, 0].reshape(count, heads_kv, head_size)
    values_part = block[:, 1].reshape(count, heads_kv, head_size)
    scores = jnp.einsum("tkgd,skd->kgts", qn, keys_part, preferred_element_type=jnp.float32)
    allowed = frames[None, :] <= text_frame[:, None]
    weights = jnp.where(allowed, jnp.exp(scores), jnp.float32(0.0))
    total = jnp.sum(weights, axis=-1)
    wb = weights.astype(jnp.bfloat16)
    summed = jnp.einsum("kgts,skd->kgtd", wb, values_part, preferred_element_type=jnp.float32)
    result = summed / total[..., None]
    return (
        result.transpose(2, 0, 1, 3)
        .reshape(text_rows, heads_kv * groups * head_size)
        .astype(jnp.bfloat16)
    )


def solution(mesh):
    return jax.shard_map(
        per_device,
        mesh=mesh,
        in_specs=(
            P(("section", "blk"), "tp"),
            P(("section", "blk")),
            P("blk", ("section", "tp")),
            P("blk"),
            P("section", None, None, "tp"),
            P("section", None),
            P("section", None),
        ),
        out_specs=P(("section", "blk"), "tp"),
        check_vma=False,
    )
```

```python
import functools

import jax
import jax.numpy as jnp
from jax import lax
from jax.experimental import pallas as pl
from jax.experimental.pallas import tpu as pltpu
from jax.sharding import PartitionSpec as P

MESH = pl.DeviceIdType.MESH
BF16 = jnp.bfloat16
F32 = jnp.float32
EPS = 1e-05


def kernel(
    dims,
    q_ref, tf_ref, x_ref, fr_ref, w_ref, qg_ref, kg_ref,
    out_ref,
    stage, kvw, xg, kv, frames, qn, acc, tot, proj,
    wsem, fsend, frecv, ssend, srecv, rsend, rrecv, zsend, zrecv,
):
    n_sec, n_blk, n_tp, n_chunk, w_rows = dims
    sec, blk, tp = lax.axis_index("section"), lax.axis_index("blk"), lax.axis_index("tp")
    par = lax.rem(sec, 2)
    half = sec // 2
    mine = half * n_tp + tp
    n_half = n_sec // 2
    n_group = n_half * n_tp
    rows, fw = x_ref.shape
    rc = rows // n_chunk
    feats, _, kv_cols = w_ref.shape[1:]
    head = qg_ref.shape[1]
    heads_kv = kv_cols // head
    text = q_ref.shape[0]
    groups = q_ref.shape[1] // kv_cols
    n_w = feats // w_rows
    n_stage = stage.shape[0]
    sibling = {"section": sec + 1 - 2 * par}

    def w_copy(i):
        return pltpu.make_async_copy(
            w_ref.at[0, pl.ds(i * w_rows, w_rows)], stage.at[i % n_stage], wsem.at[i % n_stage]
        )

    for i in range(min(n_stage, n_w)):
        w_copy(i).start()

    def plane_peer(k):
        other = lax.rem(mine + k, n_group)
        return {"section": 2 * (other // n_tp) + par, "tp": lax.rem(other, n_tp)}

    def line_peer(k):
        return {"blk": lax.rem(blk + k, n_blk)}

    barrier = pltpu.get_barrier_semaphore()
    pl.semaphore_signal(barrier, inc=1, device_id=sibling, device_id_type=MESH)
    for k in range(1, n_group):
        pl.semaphore_signal(barrier, inc=1, device_id=plane_peer(k), device_id_type=MESH)
    for k in range(1, n_blk):
        pl.semaphore_signal(barrier, inc=1, device_id=line_peer(k), device_id_type=MESH)
    pl.semaphore_wait(barrier, n_group + n_blk - 1)

    def feature_copy(c, k):
        return pltpu.make_async_remote_copy(
            src_ref=x_ref.at[pl.ds(c * rc, rc)],
            dst_ref=xg.at[c, par, mine],
            send_sem=fsend.at[c],
            recv_sem=frecv.at[c],
            device_id=plane_peer(k),
            device_id_type=MESH,
        )

    for c in range(n_chunk):
        pltpu.make_async_copy(x_ref.at[pl.ds(c * rc, rc)], xg.at[c, par, mine], frecv.at[c]).start()
        for k in range(1, n_group):
            feature_copy(c, k).start()

    def frame_copy(k):
        return pltpu.make_async_remote_copy(
            src_ref=fr_ref,
            dst_ref=frames.at[blk],
            send_sem=rsend,
            recv_sem=rrecv,
            device_id=line_peer(k),
            device_id_type=MESH,
        )

    pltpu.make_async_copy(fr_ref, frames.at[blk], rrecv).start()
    for k in range(1, n_blk):
        frame_copy(k).start()

    def share(c):
        return pltpu.make_async_remote_copy(
            src_ref=xg.at[c, par],
            dst_ref=xg.at[c, par],
            send_sem=ssend.at[c],
            recv_sem=srecv.at[c],
            device_id=sibling,
            device_id_type=MESH,
        )

    def pass_on(c):
        pltpu.make_async_copy(xg.at[c, par], xg.at[c, par], frecv.at[c]).wait()
        share(c).start()

    gain = qg_ref[...] * head ** (-0.5)

    @pl.loop(0, heads_kv)
    def _(k):
        for g in range(groups):
            col = pl.multiple_of((k * groups + g) * head, head)
            rowsq = q_ref[:, pl.ds(col, head)].astype(F32)
            scale = lax.rsqrt(jnp.mean(rowsq * rowsq, axis=-1, keepdims=True) + EPS)
            qn[k, g * text:(g + 1) * text, :] = (rowsq * scale * gain).astype(BF16)

    sub = 2 * head
    ri = lax.broadcasted_iota(jnp.int32, (sub, sub), 0)
    ci = lax.broadcasted_iota(jnp.int32, (sub, sub), 1)
    take = (ci == 2 * lax.rem(ri, head) + ri // head).astype(BF16)
    for i in range(n_w):
        w_copy(i).wait()

        @pl.loop(0, w_rows // head)
        def _(j):
            at = pl.multiple_of(j * head, head)
            block = stage[i % n_stage, pl.ds(at, head)].reshape(sub, kv_cols)
            apart = jnp.dot(take, block, preferred_element_type=F32).astype(BF16)
            to = pl.multiple_of(i * w_rows + j * head, head)
            kvw[pl.ds(to, head), :kv_cols] = apart[:head]
            kvw[pl.ds(to, head), kv_cols:] = apart[head:]

        if i + n_stage < n_w:
            w_copy(i + n_stage).start()
        if i == n_w // 2:
            pass_on(0)

    def line_copy(way, src, d, c):
        to = blk + 1 if way == 0 else blk - 1
        return pltpu.make_async_remote_copy(
            src_ref=kv.at[src, c],
            dst_ref=kv.at[src, c],
            send_sem=zsend.at[way, d - 1, c],
            recv_sem=zrecv.at[way, d - 1, c],
            device_id={"blk": to},
            device_id_type=MESH,
        )

    can = (blk + 1 < n_blk, blk >= 1)

    def source(way, d):
        return blk - d if way == 0 else blk + d

    def exists(way, d):
        return blk - d >= 0 if way == 0 else blk + d < n_blk

    def relay(way, d, c):
        @pl.when(exists(way, d))
        def _():
            src = source(way, d)
            line_copy(way, src, d, c).wait_recv()

            @pl.when(can[way])
            def _():
                line_copy(way, src, d + 1, c).start()

    for c in range(n_chunk):
        if c + 1 < n_chunk:
            pass_on(c + 1)
        share(c).wait_recv()
        proj[...] = jnp.zeros_like(proj)

        @pl.loop(0, n_group)
        def _(j):
            for p in range(2):
                place = ((2 * (j // n_tp) + p) * n_tp + lax.rem(j, n_tp)) * fw
                part = kvw[pl.ds(pl.multiple_of(place, fw), fw), :]
                proj[...] += jnp.dot(xg[c, p, j], part, preferred_element_type=F32)

        for h in range(heads_kv):
            key = proj[:, h * head:(h + 1) * head]
            scale = lax.rsqrt(jnp.mean(key * key, axis=-1, keepdims=True) + EPS)
            kv[blk, c, :, h * head:(h + 1) * head] = (key * scale * kg_ref[...]).astype(BF16)
        kv[blk, c, :, kv_cols:] = proj[:, kv_cols:].astype(BF16)
        for way in range(2):
            @pl.when(can[way])
            def _():
                line_copy(way, blk, 1, c).start()
        if c >= 1:
            for way in range(2):
                relay(way, 1, c - 1)

    pltpu.make_async_copy(frames, frames, rrecv).wait()
    limit = jnp.broadcast_to(tf_ref[...], (text, text)).T[:, :1]
    acc[...] = jnp.zeros_like(acc)
    tot[...] = jnp.zeros_like(tot)

    def attend(src):
        allowed = frames[src] <= limit

        @pl.loop(0, heads_kv)
        def _(k):
            at = pl.multiple_of(k * head, head)
            keys = kv[src, :, :, pl.ds(at, head)].reshape(rows, head)
            values = kv[src, :, :, pl.ds(kv_cols + at, head)].reshape(rows, head)
            for g in range(groups):
                span = slice(g * text, (g + 1) * text)
                scores = lax.dot_general(
                    qn[k, span, :], keys, (((1,), (1,)), ((), ())), preferred_element_type=F32
                )
                weights = jnp.where(allowed, jnp.exp(scores), 0.0)
                total = weights[:, :head]
                for m in range(1, rows // head):
                    total = total + weights[:, m * head:(m + 1) * head]
                tot[k, span, :] += total
                acc[k, span, :] += jnp.dot(
                    weights.astype(BF16), values, preferred_element_type=F32
                )

    def attend_if(way, d):
        @pl.when(exists(way, d))
        def _():
            attend(source(way, d))

    for way in range(2):
        relay(way, 1, n_chunk - 1)
    attend(blk)

    @pl.loop(1, n_blk - 1)
    def _(d):
        for c in range(n_chunk):
            for way in range(2):
                relay(way, d + 1, c)
        for way in range(2):
            attend_if(way, d)

    for way in range(2):
        attend_if(way, n_blk - 1)

    @pl.loop(0, heads_kv)
    def _(k):
        for g in range(groups):
            span = slice(g * text, (g + 1) * text)
            total = jnp.sum(tot[k, span, :], axis=-1, keepdims=True)
            col = pl.multiple_of((k * groups + g) * head, head)
            out_ref[:, pl.ds(col, head)] = (acc[k, span, :] / total).astype(BF16)

    for c in range(n_chunk):
        if n_group > 1:
            gone = xg.at[c, par, pl.ds(0, n_group - 1)]
            pltpu.make_async_copy(gone, gone, fsend.at[c]).wait()
        share(c).wait_send()
    if n_blk > 1:
        gone = frames.at[pl.ds(0, n_blk - 1)]
        pltpu.make_async_copy(gone, gone, rsend).wait()

    @pl.loop(1, n_blk)
    def _(d):
        for way in range(2):
            @pl.when(can[way] & exists(way, d - 1))
            def _():
                for c in range(n_chunk):
                    line_copy(way, source(way, d - 1), d, c).wait_send()


def solution(mesh):
    n_sec, n_blk, n_tp = mesh.shape["section"], mesh.shape["blk"], mesh.shape["tp"]

    def per_device(query, text_frame, image_feats, image_frame, kv_weight, query_gain, key_gain):
        text = query.shape[0]
        rows, fw = image_feats.shape
        feats, _, kv_cols = kv_weight.shape[1:]
        head = query_gain.shape[1]
        heads_kv = kv_cols // head
        groups = query.shape[1] // kv_cols
        n_chunk = 4
        rc = rows // n_chunk
        w_rows = 1024
        n_stage = 4
        n_group = n_sec // 2 * n_tp
        vmem = pl.BlockSpec(memory_space=pltpu.VMEM)
        dma = pltpu.SemaphoreType.DMA
        return pl.pallas_call(
            functools.partial(kernel, (n_sec, n_blk, n_tp, n_chunk, w_rows)),
            out_shape=jax.ShapeDtypeStruct(query.shape, BF16),
            in_specs=[vmem, vmem, vmem, vmem, pl.BlockSpec(memory_space=pl.ANY), vmem, vmem],
            out_specs=vmem,
            scratch_shapes=[
                pltpu.VMEM((n_stage, w_rows, 2, kv_cols), BF16),
                pltpu.VMEM((feats, 2 * kv_cols), BF16),
                pltpu.VMEM((n_chunk, 2, n_group, rc, fw), BF16),
                pltpu.VMEM((n_blk, n_chunk, rc, 2 * kv_cols), BF16),
                pltpu.VMEM((n_blk, 1, rows), jnp.int32),
                pltpu.VMEM((heads_kv, groups * text, head), BF16),
                pltpu.VMEM((heads_kv, groups * text, head), F32),
                pltpu.VMEM((heads_kv, groups * text, head), F32),
                pltpu.VMEM((rc, 2 * kv_cols), F32),
                dma((n_stage,)),
                dma((n_chunk,)),
                dma((n_chunk,)),
                dma((n_chunk,)),
                dma((n_chunk,)),
                dma,
                dma,
                dma((2, n_blk, n_chunk)),
                dma((2, n_blk, n_chunk)),
            ],
            compiler_params=pltpu.CompilerParams(
                collective_id=0, has_side_effects=True, vmem_limit_bytes=56 << 20
            ),
        )(
            query,
            text_frame.reshape(1, text),
            image_feats,
            image_frame.reshape(1, rows),
            kv_weight,
            query_gain,
            key_gain,
        )

    return jax.shard_map(
        per_device,
        mesh=mesh,
        in_specs=(
            P(("section", "blk"), "tp"),
            P(("section", "blk")),
            P("blk", ("section", "tp")),
            P("blk"),
            P("section", None, None, "tp"),
            P("section", None),
            P("section", None),
        ),
        out_specs=P(("section", "blk"), "tp"),
        check_vma=False,
    )
```

```python
import functools

import jax
import jax.numpy as jnp
from jax import lax
from jax.experimental import pallas as pl
from jax.experimental.pallas import tpu as pltpu
from jax.sharding import PartitionSpec as P

MESH = pl.DeviceIdType.MESH
BF16 = jnp.bfloat16
F32 = jnp.float32
EPS = 1e-05


def kernel(
    dims,
    q_ref, tf_ref, x_ref, fr_ref, w_ref, qg_ref, kg_ref,
    out_ref,
    stage, kvw, xg, kv, frames, qn, acc, tot, proj,
    wsem, fsend, frecv, ssend, srecv, rsend, rrecv, zsend, zrecv,
):
    n_sec, n_blk, n_tp, n_chunk, w_rows = dims
    sec, blk, tp = lax.axis_index("section"), lax.axis_index("blk"), lax.axis_index("tp")
    par = lax.rem(sec, 2)
    half = sec // 2
    mine = half * n_tp + tp
    n_half = n_sec // 2
    n_group = n_half * n_tp
    rows, fw = x_ref.shape
    rc = rows // n_chunk
    feats, _, kv_cols = w_ref.shape[1:]
    head = qg_ref.shape[1]
    heads_kv = kv_cols // head
    text = q_ref.shape[0]
    groups = q_ref.shape[1] // kv_cols
    n_w = feats // w_rows
    n_stage = stage.shape[0]
    sibling = {"section": sec + 1 - 2 * par}

    def w_copy(i):
        return pltpu.make_async_copy(
            w_ref.at[0, pl.ds(i * w_rows, w_rows)], stage.at[i % n_stage], wsem.at[i % n_stage]
        )

    for i in range(min(n_stage, n_w)):
        w_copy(i).start()

    def plane_peer(k):
        other = lax.rem(mine + k, n_group)
        return {"section": 2 * (other // n_tp) + par, "tp": lax.rem(other, n_tp)}

    def line_peer(k):
        return {"blk": lax.rem(blk + k, n_blk)}

    barrier = pltpu.get_barrier_semaphore()
    pl.semaphore_signal(barrier, inc=1, device_id=sibling, device_id_type=MESH)
    for k in range(1, n_group):
        pl.semaphore_signal(barrier, inc=1, device_id=plane_peer(k), device_id_type=MESH)
    for k in range(1, n_blk):
        pl.semaphore_signal(barrier, inc=1, device_id=line_peer(k), device_id_type=MESH)
    pl.semaphore_wait(barrier, n_group + n_blk - 1)

    square = n_half == 2 and n_tp == 2
    near = ({"section": 2 * (1 - half) + par}, {"tp": 1 - tp})
    near_at = ((1 - half) * n_tp + tp, half * n_tp + 1 - tp)

    def feature_copy(c, k):
        return pltpu.make_async_remote_copy(
            src_ref=x_ref.at[pl.ds(c * rc, rc)],
            dst_ref=xg.at[c, par, mine],
            send_sem=fsend.at[c, k if square else 0],
            recv_sem=frecv.at[c, k if square else 2],
            device_id=near[k] if square else plane_peer(k),
            device_id_type=MESH,
        )

    def arrived(c, k):
        return pltpu.make_async_remote_copy(
            src_ref=x_ref.at[pl.ds(c * rc, rc)],
            dst_ref=xg.at[c, par, near_at[k]],
            send_sem=fsend.at[c, k],
            recv_sem=frecv.at[c, k],
            device_id=near[k],
            device_id_type=MESH,
        )

    def corner_copy(c, k, at):
        part = xg.at[c, par, at, pl.ds(k * (rc // 2), rc // 2)]
        return pltpu.make_async_remote_copy(
            src_ref=part,
            dst_ref=part,
            send_sem=fsend.at[c, 2 + k],
            recv_sem=frecv.at[c, 3 + k],
            device_id=near[1 - k],
            device_id_type=MESH,
        )

    def local_copy(c):
        return pltpu.make_async_copy(
            x_ref.at[pl.ds(c * rc, rc)], xg.at[c, par, mine], frecv.at[c, 2]
        )

    def start(c):
        for k in range(2) if square else range(1, n_group):
            feature_copy(c, k).start()
        local_copy(c).start()

    def forward(c):
        if square:
            for k in range(2):
                arrived(c, k).wait_recv()
                corner_copy(c, k, near_at[k]).start()

    start(0)
    if n_chunk > 1:
        start(1)

    def frame_copy(k):
        return pltpu.make_async_remote_copy(
            src_ref=fr_ref,
            dst_ref=frames.at[blk],
            send_sem=rsend,
            recv_sem=rrecv,
            device_id=line_peer(k),
            device_id_type=MESH,
        )

    pltpu.make_async_copy(fr_ref, frames.at[blk], rrecv).start()
    for k in range(1, n_blk):
        frame_copy(k).start()

    def share(c):
        return pltpu.make_async_remote_copy(
            src_ref=xg.at[c, par],
            dst_ref=xg.at[c, par],
            send_sem=ssend.at[c],
            recv_sem=srecv.at[c],
            device_id=sibling,
            device_id_type=MESH,
        )

    def pass_on(c):
        if square:
            local_copy(c).wait()
            for k in range(2):
                corner_copy(c, k, (1 - half) * n_tp + 1 - tp).wait_recv()
        else:
            pltpu.make_async_copy(xg.at[c, par], xg.at[c, par], frecv.at[c, 2]).wait()
        share(c).start()

    sub = 2 * head
    ri = lax.broadcasted_iota(jnp.int32, (sub, sub), 0)
    ci = lax.broadcasted_iota(jnp.int32, (sub, sub), 1)
    take = (ci == 2 * lax.rem(ri, head) + ri // head).astype(BF16)
    for i in range(n_w):
        w_copy(i).wait()

        @pl.loop(0, w_rows // head, unroll=4)
        def _(j):
            at = pl.multiple_of(j * head, head)
            block = stage[i % n_stage, pl.ds(at, head)].reshape(sub, kv_cols)
            apart = jnp.dot(take, block, preferred_element_type=F32).astype(BF16)
            to = pl.multiple_of(i * w_rows + j * head, head)
            kvw[pl.ds(to, head), :kv_cols] = apart[:head]
            kvw[pl.ds(to, head), kv_cols:] = apart[head:]

        if i + n_stage < n_w:
            w_copy(i + n_stage).start()
        if i == n_w // 8:
            forward(0)
            if n_chunk > 2:
                start(2)
        if i == (3 * n_w) // 8:
            pass_on(0)
        if i == (5 * n_w) // 8 and n_chunk > 1:
            forward(1)
            if n_chunk > 3:
                start(3)

    def line_copy(way, src, d, c):
        to = blk + 1 if way == 0 else blk - 1
        return pltpu.make_async_remote_copy(
            src_ref=kv.at[src, c],
            dst_ref=kv.at[src, c],
            send_sem=zsend.at[way, d - 1, c],
            recv_sem=zrecv.at[way, d - 1, c],
            device_id={"blk": to},
            device_id_type=MESH,
        )

    can = (blk + 1 < n_blk, blk >= 1)

    def source(way, d):
        return blk - d if way == 0 else blk + d

    def exists(way, d):
        return blk - d >= 0 if way == 0 else blk + d < n_blk

    def relay(way, d, c):
        @pl.when(exists(way, d))
        def _():
            src = source(way, d)
            line_copy(way, src, d, c).wait_recv()

            @pl.when(can[way])
            def _():
                line_copy(way, src, d + 1, c).start()

    for c in range(n_chunk):
        share(c).wait_recv()
        proj[...] = jnp.zeros_like(proj)

        @pl.loop(0, n_group)
        def _(j):
            for p in range(2):
                place = ((2 * (j // n_tp) + p) * n_tp + lax.rem(j, n_tp)) * fw
                part = kvw[pl.ds(pl.multiple_of(place, fw), fw), :]
                proj[...] += jnp.dot(xg[c, p, j], part, preferred_element_type=F32)

        for h in range(heads_kv):
            key = proj[:, h * head:(h + 1) * head]
            scale = lax.rsqrt(jnp.mean(key * key, axis=-1, keepdims=True) + EPS)
            kv[blk, c, :, h * head:(h + 1) * head] = (key * scale * kg_ref[...]).astype(BF16)
        kv[blk, c, :, kv_cols:] = proj[:, kv_cols:].astype(BF16)
        for way in range(2):
            @pl.when(can[way])
            def _():
                line_copy(way, blk, 1, c).start()
        if c + 1 < n_chunk:
            pass_on(c + 1)
        if c + 2 < n_chunk:
            forward(c + 2)
        if c + 4 < n_chunk:
            start(c + 4)
        if c >= 1:
            for way in range(2):
                relay(way, 1, c - 1)

    gain = qg_ref[...] * head ** (-0.5)

    @pl.loop(0, heads_kv)
    def _(k):
        for g in range(groups):
            col = pl.multiple_of((k * groups + g) * head, head)
            rowsq = q_ref[:, pl.ds(col, head)].astype(F32)
            scale = lax.rsqrt(jnp.mean(rowsq * rowsq, axis=-1, keepdims=True) + EPS)
            qn[k, g * text:(g + 1) * text, :] = (rowsq * scale * gain).astype(BF16)

    pltpu.make_async_copy(frames, frames, rrecv).wait()
    limit = jnp.broadcast_to(tf_ref[...], (text, text)).T[:, :1]
    acc[...] = jnp.zeros_like(acc)
    tot[...] = jnp.zeros_like(tot)

    def attend(src):
        allowed = frames[src] <= limit

        @pl.loop(0, heads_kv)
        def _(k):
            at = pl.multiple_of(k * head, head)
            keys = kv[src, :, :, pl.ds(at, head)].reshape(rows, head)
            values = kv[src, :, :, pl.ds(kv_cols + at, head)].reshape(rows, head)
            for g in range(groups):
                span = slice(g * text, (g + 1) * text)
                scores = lax.dot_general(
                    qn[k, span, :], keys, (((1,), (1,)), ((), ())), preferred_element_type=F32
                )
                weights = jnp.where(allowed, jnp.exp(scores), 0.0)
                total = weights[:, :head]
                for m in range(1, rows // head):
                    total = total + weights[:, m * head:(m + 1) * head]
                tot[k, span, :] += total
                acc[k, span, :] += jnp.dot(
                    weights.astype(BF16), values, preferred_element_type=F32
                )

    def attend_if(way, d):
        @pl.when(exists(way, d))
        def _():
            attend(source(way, d))

    for way in range(2):
        relay(way, 1, n_chunk - 1)
    attend(blk)

    @pl.loop(1, n_blk - 1)
    def _(d):
        for c in range(n_chunk):
            for way in range(2):
                relay(way, d + 1, c)
            if c < 2:
                attend_if(c, d)

    for way in range(2):
        attend_if(way, n_blk - 1)

    @pl.loop(0, heads_kv)
    def _(k):
        for g in range(groups):
            span = slice(g * text, (g + 1) * text)
            total = jnp.sum(tot[k, span, :], axis=-1, keepdims=True)
            col = pl.multiple_of((k * groups + g) * head, head)
            out_ref[:, pl.ds(col, head)] = (acc[k, span, :] / total).astype(BF16)

    for c in range(n_chunk):
        if square:
            for k in range(2):
                feature_copy(c, k).wait_send()
                corner_copy(c, k, near_at[k]).wait_send()
        elif n_group > 1:
            gone = xg.at[c, par, pl.ds(0, n_group - 1)]
            pltpu.make_async_copy(gone, gone, fsend.at[c, 0]).wait()
        share(c).wait_send()
    if n_blk > 1:
        gone = frames.at[pl.ds(0, n_blk - 1)]
        pltpu.make_async_copy(gone, gone, rsend).wait()

    @pl.loop(1, n_blk)
    def _(d):
        for way in range(2):
            @pl.when(can[way] & exists(way, d - 1))
            def _():
                for c in range(n_chunk):
                    line_copy(way, source(way, d - 1), d, c).wait_send()


def solution(mesh):
    n_sec, n_blk, n_tp = mesh.shape["section"], mesh.shape["blk"], mesh.shape["tp"]

    def per_device(query, text_frame, image_feats, image_frame, kv_weight, query_gain, key_gain):
        text = query.shape[0]
        rows, fw = image_feats.shape
        feats, _, kv_cols = kv_weight.shape[1:]
        head = query_gain.shape[1]
        heads_kv = kv_cols // head
        groups = query.shape[1] // kv_cols
        n_chunk = 4
        rc = rows // n_chunk
        w_rows = 1024
        n_stage = 4
        n_group = n_sec // 2 * n_tp
        vmem = pl.BlockSpec(memory_space=pltpu.VMEM)
        dma = pltpu.SemaphoreType.DMA
        return pl.pallas_call(
            functools.partial(kernel, (n_sec, n_blk, n_tp, n_chunk, w_rows)),
            out_shape=jax.ShapeDtypeStruct(query.shape, BF16),
            in_specs=[vmem, vmem, vmem, vmem, pl.BlockSpec(memory_space=pl.ANY), vmem, vmem],
            out_specs=vmem,
            scratch_shapes=[
                pltpu.VMEM((n_stage, w_rows, 2, kv_cols), BF16),
                pltpu.VMEM((feats, 2 * kv_cols), BF16),
                pltpu.VMEM((n_chunk, 2, n_group, rc, fw), BF16),
                pltpu.VMEM((n_blk, n_chunk, rc, 2 * kv_cols), BF16),
                pltpu.VMEM((n_blk, 1, rows), jnp.int32),
                pltpu.VMEM((heads_kv, groups * text, head), BF16),
                pltpu.VMEM((heads_kv, groups * text, head), F32),
                pltpu.VMEM((heads_kv, groups * text, head), F32),
                pltpu.VMEM((rc, 2 * kv_cols), F32),
                dma((n_stage,)),
                dma((n_chunk, 4)),
                dma((n_chunk, 5)),
                dma((n_chunk,)),
                dma((n_chunk,)),
                dma,
                dma,
                dma((2, n_blk, n_chunk)),
                dma((2, n_blk, n_chunk)),
            ],
            compiler_params=pltpu.CompilerParams(
                collective_id=0, has_side_effects=True, vmem_limit_bytes=56 << 20
            ),
        )(
            query,
            text_frame.reshape(1, text),
            image_feats,
            image_frame.reshape(1, rows),
            kv_weight,
            query_gain,
            key_gain,
        )

    return jax.shard_map(
        per_device,
        mesh=mesh,
        in_specs=(
            P(("section", "blk"), "tp"),
            P(("section", "blk")),
            P("blk", ("section", "tp")),
            P("blk"),
            P("section", None, None, "tp"),
            P("section", None),
            P("section", None),
        ),
        out_specs=P(("section", "blk"), "tp"),
        check_vma=False,
    )
```

```python
import functools

import jax
import jax.numpy as jnp
from jax import lax
from jax.experimental import pallas as pl
from jax.experimental.pallas import tpu as pltpu
from jax.sharding import PartitionSpec as P

MESH = pl.DeviceIdType.MESH
BF16 = jnp.bfloat16
F32 = jnp.float32
EPS = 1e-05


def kernel(
    dims,
    q_ref, tf_ref, x_ref, fr_ref, w_ref, qg_ref, kg_ref,
    out_ref,
    stage, kvw, xg, kv, frames, qn, acc, tot, proj,
    wsem, fsend, frecv, ssend, srecv, rsend, rrecv, zsend, zrecv,
):
    n_sec, n_blk, n_tp, n_chunk, w_rows = dims
    sec, blk, tp = lax.axis_index("section"), lax.axis_index("blk"), lax.axis_index("tp")
    par = lax.rem(sec, 2)
    half = sec // 2
    mine = half * n_tp + tp
    n_half = n_sec // 2
    n_group = n_half * n_tp
    rows, fw = x_ref.shape
    rc = rows // n_chunk
    feats, _, kv_cols = w_ref.shape[1:]
    head = qg_ref.shape[1]
    heads_kv = kv_cols // head
    text = q_ref.shape[0]
    groups = q_ref.shape[1] // kv_cols
    n_w = feats // w_rows
    n_stage = stage.shape[0]
    sibling = {"section": sec + 1 - 2 * par}

    def w_copy(i):
        return pltpu.make_async_copy(
            w_ref.at[0, pl.ds(i * w_rows, w_rows)], stage.at[i % n_stage], wsem.at[i % n_stage]
        )

    for i in range(min(n_stage, n_w)):
        w_copy(i).start()

    def plane_peer(k):
        other = lax.rem(mine + k, n_group)
        return {"section": 2 * (other // n_tp) + par, "tp": lax.rem(other, n_tp)}

    def line_peer(k):
        return {"blk": lax.rem(blk + k, n_blk)}

    barrier = pltpu.get_barrier_semaphore()
    pl.semaphore_signal(barrier, inc=1, device_id=sibling, device_id_type=MESH)
    for k in range(1, n_group):
        pl.semaphore_signal(barrier, inc=1, device_id=plane_peer(k), device_id_type=MESH)
    for k in range(1, n_blk):
        pl.semaphore_signal(barrier, inc=1, device_id=line_peer(k), device_id_type=MESH)
    pl.semaphore_wait(barrier, n_group + n_blk - 1)

    square = n_half == 2 and n_tp == 2
    near = ({"section": 2 * (1 - half) + par}, {"tp": 1 - tp})
    near_at = ((1 - half) * n_tp + tp, half * n_tp + 1 - tp)

    def feature_copy(c, k):
        return pltpu.make_async_remote_copy(
            src_ref=x_ref.at[pl.ds(c * rc, rc)],
            dst_ref=xg.at[c, par, mine],
            send_sem=fsend.at[c, k if square else 0],
            recv_sem=frecv.at[c, k if square else 2],
            device_id=near[k] if square else plane_peer(k),
            device_id_type=MESH,
        )

    def arrived(c, k):
        return pltpu.make_async_remote_copy(
            src_ref=x_ref.at[pl.ds(c * rc, rc)],
            dst_ref=xg.at[c, par, near_at[k]],
            send_sem=fsend.at[c, k],
            recv_sem=frecv.at[c, k],
            device_id=near[k],
            device_id_type=MESH,
        )

    def corner_copy(c, k, at):
        part = xg.at[c, par, at, pl.ds(k * (rc // 2), rc // 2)]
        return pltpu.make_async_remote_copy(
            src_ref=part,
            dst_ref=part,
            send_sem=fsend.at[c, 2 + k],
            recv_sem=frecv.at[c, 3 + k],
            device_id=near[1 - k],
            device_id_type=MESH,
        )

    def local_copy(c):
        return pltpu.make_async_copy(
            x_ref.at[pl.ds(c * rc, rc)], xg.at[c, par, mine], frecv.at[c, 2]
        )

    def start(c):
        for k in range(2) if square else range(1, n_group):
            feature_copy(c, k).start()
        local_copy(c).start()

    def forward(c):
        if square:
            for k in range(2):
                arrived(c, k).wait_recv()
                corner_copy(c, k, near_at[k]).start()

    start(0)
    if n_chunk > 1:
        start(1)

    def frame_copy(k):
        return pltpu.make_async_remote_copy(
            src_ref=fr_ref,
            dst_ref=frames.at[blk],
            send_sem=rsend,
            recv_sem=rrecv,
            device_id=line_peer(k),
            device_id_type=MESH,
        )

    pltpu.make_async_copy(fr_ref, frames.at[blk], rrecv).start()
    for k in range(1, n_blk):
        frame_copy(k).start()

    def share(c):
        return pltpu.make_async_remote_copy(
            src_ref=xg.at[c, par],
            dst_ref=xg.at[c, par],
            send_sem=ssend.at[c],
            recv_sem=srecv.at[c],
            device_id=sibling,
            device_id_type=MESH,
        )

    def pass_on(c):
        if square:
            local_copy(c).wait()
            for k in range(2):
                corner_copy(c, k, (1 - half) * n_tp + 1 - tp).wait_recv()
        else:
            pltpu.make_async_copy(xg.at[c, par], xg.at[c, par], frecv.at[c, 2]).wait()
        share(c).start()

    sub = 2 * head
    ri = lax.broadcasted_iota(jnp.int32, (sub, sub), 0)
    ci = lax.broadcasted_iota(jnp.int32, (sub, sub), 1)
    take = (ci == 2 * lax.rem(ri, head) + ri // head).astype(BF16)
    for i in range(n_w):
        w_copy(i).wait()

        @pl.loop(0, w_rows // head, unroll=4)
        def _(j):
            at = pl.multiple_of(j * head, head)
            block = stage[i % n_stage, pl.ds(at, head)].reshape(sub, kv_cols)
            apart = jnp.dot(take, block, preferred_element_type=F32).astype(BF16)
            to = pl.multiple_of(i * w_rows + j * head, head)
            kvw[pl.ds(to, head), :kv_cols] = apart[:head]
            kvw[pl.ds(to, head), kv_cols:] = apart[head:]

        if i + n_stage < n_w:
            w_copy(i + n_stage).start()
        if i == n_w // 8:
            forward(0)
            if n_chunk > 2:
                start(2)
        if i == (3 * n_w) // 8:
            pass_on(0)
        if i == (5 * n_w) // 8 and n_chunk > 1:
            forward(1)
            if n_chunk > 3:
                start(3)

    def line_copy(way, src, d, c):
        to = blk + 1 if way == 0 else blk - 1
        return pltpu.make_async_remote_copy(
            src_ref=kv.at[src, c],
            dst_ref=kv.at[src, c],
            send_sem=zsend.at[way, d - 1, c],
            recv_sem=zrecv.at[way, d - 1, c],
            device_id={"blk": to},
            device_id_type=MESH,
        )

    can = (blk + 1 < n_blk, blk >= 1)

    def source(way, d):
        return blk - d if way == 0 else blk + d

    def exists(way, d):
        return blk - d >= 0 if way == 0 else blk + d < n_blk

    def relay(way, d, c):
        @pl.when(exists(way, d))
        def _():
            src = source(way, d)
            line_copy(way, src, d, c).wait_recv()

            @pl.when(can[way])
            def _():
                line_copy(way, src, d + 1, c).start()

    for c in range(n_chunk):
        share(c).wait_recv()
        proj[...] = jnp.zeros_like(proj)

        @pl.loop(0, n_group, unroll=2)
        def _(j):
            for p in range(2):
                place = ((2 * (j // n_tp) + p) * n_tp + lax.rem(j, n_tp)) * fw
                part = kvw[pl.ds(pl.multiple_of(place, fw), fw), :]
                proj[...] += jnp.dot(xg[c, p, j], part, preferred_element_type=F32)

        for h in range(heads_kv):
            key = proj[:, h * head:(h + 1) * head]
            scale = lax.rsqrt(jnp.mean(key * key, axis=-1, keepdims=True) + EPS)
            kv[blk, c, :, h * head:(h + 1) * head] = (key * scale * kg_ref[...]).astype(BF16)
        kv[blk, c, :, kv_cols:] = proj[:, kv_cols:].astype(BF16)
        for way in range(2):
            @pl.when(can[way])
            def _():
                line_copy(way, blk, 1, c).start()
        if c + 1 < n_chunk:
            pass_on(c + 1)
        if c >= 1:
            for way in range(2):
                relay(way, 1, c - 1)
        if c + 2 < n_chunk:
            forward(c + 2)
        if c + 4 < n_chunk:
            start(c + 4)

    gain = qg_ref[...] * head ** (-0.5)

    @pl.loop(0, heads_kv)
    def _(k):
        for g in range(groups):
            col = pl.multiple_of((k * groups + g) * head, head)
            rowsq = q_ref[:, pl.ds(col, head)].astype(F32)
            scale = lax.rsqrt(jnp.mean(rowsq * rowsq, axis=-1, keepdims=True) + EPS)
            qn[k, g * text:(g + 1) * text, :] = (rowsq * scale * gain).astype(BF16)

    pltpu.make_async_copy(frames, frames, rrecv).wait()
    limit = jnp.broadcast_to(tf_ref[...], (text, text)).T[:, :1]
    acc[...] = jnp.zeros_like(acc)
    tot[...] = jnp.zeros_like(tot)

    def attend(src):
        allowed = frames[src] <= limit

        @pl.loop(0, heads_kv)
        def _(k):
            at = pl.multiple_of(k * head, head)
            keys = kv[src, :, :, pl.ds(at, head)].reshape(rows, head)
            values = kv[src, :, :, pl.ds(kv_cols + at, head)].reshape(rows, head)
            for g in range(groups):
                span = slice(g * text, (g + 1) * text)
                scores = lax.dot_general(
                    qn[k, span, :], keys, (((1,), (1,)), ((), ())), preferred_element_type=F32
                )
                weights = jnp.where(allowed, jnp.exp(scores), 0.0)
                total = weights[:, :head]
                for m in range(1, rows // head):
                    total = total + weights[:, m * head:(m + 1) * head]
                tot[k, span, :] += total
                acc[k, span, :] += jnp.dot(
                    weights.astype(BF16), values, preferred_element_type=F32
                )

    def attend_if(way, d):
        @pl.when(exists(way, d))
        def _():
            attend(source(way, d))

    for way in range(2):
        relay(way, 1, n_chunk - 1)
    attend(blk)

    @pl.loop(1, n_blk - 1)
    def _(d):
        for c in range(n_chunk):
            for way in range(2):
                relay(way, d + 1, c)
            if c < 2:
                attend_if(c, d)

    for way in range(2):
        attend_if(way, n_blk - 1)

    @pl.loop(0, heads_kv)
    def _(k):
        for g in range(groups):
            span = slice(g * text, (g + 1) * text)
            total = jnp.sum(tot[k, span, :], axis=-1, keepdims=True)
            col = pl.multiple_of((k * groups + g) * head, head)
            out_ref[:, pl.ds(col, head)] = (acc[k, span, :] / total).astype(BF16)

    for c in range(n_chunk):
        if square:
            for k in range(2):
                feature_copy(c, k).wait_send()
                corner_copy(c, k, near_at[k]).wait_send()
        elif n_group > 1:
            gone = xg.at[c, par, pl.ds(0, n_group - 1)]
            pltpu.make_async_copy(gone, gone, fsend.at[c, 0]).wait()
        share(c).wait_send()
    if n_blk > 1:
        gone = frames.at[pl.ds(0, n_blk - 1)]
        pltpu.make_async_copy(gone, gone, rsend).wait()

    @pl.loop(1, n_blk)
    def _(d):
        for way in range(2):
            @pl.when(can[way] & exists(way, d - 1))
            def _():
                for c in range(n_chunk):
                    line_copy(way, source(way, d - 1), d, c).wait_send()


def solution(mesh):
    n_sec, n_blk, n_tp = mesh.shape["section"], mesh.shape["blk"], mesh.shape["tp"]

    def per_device(query, text_frame, image_feats, image_frame, kv_weight, query_gain, key_gain):
        text = query.shape[0]
        rows, fw = image_feats.shape
        feats, _, kv_cols = kv_weight.shape[1:]
        head = query_gain.shape[1]
        heads_kv = kv_cols // head
        groups = query.shape[1] // kv_cols
        n_chunk = 4
        rc = rows // n_chunk
        w_rows = 1024
        n_stage = 4
        n_group = n_sec // 2 * n_tp
        vmem = pl.BlockSpec(memory_space=pltpu.VMEM)
        dma = pltpu.SemaphoreType.DMA
        return pl.pallas_call(
            functools.partial(kernel, (n_sec, n_blk, n_tp, n_chunk, w_rows)),
            out_shape=jax.ShapeDtypeStruct(query.shape, BF16),
            in_specs=[vmem, vmem, vmem, vmem, pl.BlockSpec(memory_space=pl.ANY), vmem, vmem],
            out_specs=vmem,
            scratch_shapes=[
                pltpu.VMEM((n_stage, w_rows, 2, kv_cols), BF16),
                pltpu.VMEM((feats, 2 * kv_cols), BF16),
                pltpu.VMEM((n_chunk, 2, n_group, rc, fw), BF16),
                pltpu.VMEM((n_blk, n_chunk, rc, 2 * kv_cols), BF16),
                pltpu.VMEM((n_blk, 1, rows), jnp.int32),
                pltpu.VMEM((heads_kv, groups * text, head), BF16),
                pltpu.VMEM((heads_kv, groups * text, head), F32),
                pltpu.VMEM((heads_kv, groups * text, head), F32),
                pltpu.VMEM((rc, 2 * kv_cols), F32),
                dma((n_stage,)),
                dma((n_chunk, 4)),
                dma((n_chunk, 5)),
                dma((n_chunk,)),
                dma((n_chunk,)),
                dma,
                dma,
                dma((2, n_blk, n_chunk)),
                dma((2, n_blk, n_chunk)),
            ],
            compiler_params=pltpu.CompilerParams(
                collective_id=0, has_side_effects=True, vmem_limit_bytes=56 << 20
            ),
        )(
            query,
            text_frame.reshape(1, text),
            image_feats,
            image_frame.reshape(1, rows),
            kv_weight,
            query_gain,
            key_gain,
        )

    return jax.shard_map(
        per_device,
        mesh=mesh,
        in_specs=(
            P(("section", "blk"), "tp"),
            P(("section", "blk")),
            P("blk", ("section", "tp")),
            P("blk"),
            P("section", None, None, "tp"),
            P("section", None),
            P("section", None),
        ),
        out_specs=P(("section", "blk"), "tp"),
        check_vma=False,
    )
```
